512 devices in a mesh: dp: 32 (over z_lo, y, core), ctx: 16 (over z_hi, x).
Axes of the slice: x: 4, y: 8, z: 8 (z_hi: 4, z_lo: 2; z = z_hi * 2 + z_lo), core: 2. Of those that a mesh axis runs over, the one named last changes fastest.
Arguments:
- output_gradient: float32 [32, 8, 131072], P('dp', None, 'ctx'), may hold values from -6 to 6
- input_spectrum: float32 [32, 8, 2, 131072], P('dp', None, None, 'ctx'), may hold values from -0.013671875 to 0.013671875
- filter_spectrum: float32 [8, 2, 131072], P(None, None, 'ctx'), may hold values from -12 to 12
Outputs:
- input_gradient: float32 [32, 8, 131072], P('dp', None, 'ctx')
- filter_gradient: float32 [8, 2, 131072], P(None, None, ('ctx', 'dp'))
The draws below stay inside these ranges and needn't reach their ends.
All inputs are finite; a program needn't handle non-finite values.
Results may differ from the reference program's by a relative error of at most 0.0001.
Values sent between devices are 32-bit elements; how exact they have to be, the bound alone decides.
No kernel may reach another device: no remote copies, remote signals or barrier semaphores. Data moves between devices by JAX's collectives and lax.ppermute only.
A program may use at most 128 MiB of HBM per device.

```python
import jax
import jax.numpy as jnp
from jax import lax

CHANS = 8
TOK_DEV = 8192
LEN = 131072
BATCH = 32
SECTIONS = 4
N_CTX = 16


def strengthened(array, key, source, target, blocks, factor):
    owner, partner = [(jnp.arange(array.shape[position]) // (array.shape[position] // blocks)).reshape([-1 if axis == position else 1 for axis in range(array.ndim)]) for position in (source, target)]
    chosen = jax.random.permutation(key, blocks)[partner]
    strong = (owner == chosen) | (owner == (partner + blocks // 2) % blocks)
    return jnp.where(strong, factor * array, array)


def level_of(key, extent, cuts, low, top_value):
    def one(dim, shards_of):
        draws = jax.random.uniform(jax.random.fold_in(jax.random.fold_in(key, 6), dim), (shards_of,), jnp.float32, low / len(cuts), top_value / len(cuts))
        return jnp.repeat(jnp.exp(draws), extent[dim] // shards_of).reshape((-1,) + (1,) * (len(extent) - dim - 1))

    loudness = one(*cuts[0])
    for cut in cuts[1:]:
        loudness = loudness * one(*cut)
    return loudness


def bell_draw(key, shape, scale, most, cuts=(), held_as=jnp.bfloat16):
    entries = jax.random.normal(key, shape, jnp.float32) * scale
    if len(cuts) > 0:
        entries = level_of(key, shape, cuts, -0.22, 0.18) * entries
    return jnp.clip(entries, min=-most, max=most).astype(held_as)


def gaussian_with(rng, dims, width, limit, split, heavy, held_as=jnp.bfloat16):
    values = width * jax.random.normal(rng, dims, jnp.float32)
    if split:
        values = values * level_of(rng, dims, split, -0.22, 0.18)
    return jnp.clip(strengthened(values, jax.random.fold_in(rng, 3), *heavy), -limit, limit).astype(held_as)


def setup_inputs(seed: int = 0) -> dict:
    seeds = jax.random.split(jax.random.key(seed), 4)
    return {
        "output_gradient": bell_draw(seeds[0], (BATCH, CHANS, LEN), 1.0, 6.0, ((0, 32), (2, 16)), jnp.float32),
        "input_spectrum": gaussian_with(seeds[1], (BATCH, CHANS, 2, LEN), ((LEN * BATCH) ** -0.5), 0.013671875, ((0, 32), (3, 16)), (0, 3, 32, 2.75), jnp.float32),
        "filter_spectrum": bell_draw(seeds[2], (CHANS, 2, LEN), 2.0, 12.0, ((2, 16),), jnp.float32),
    }


def reverse_digits(index):
    result = jnp.zeros_like(index)
    for level in range(SECTIONS):
        result = result | (((index >> level) & 1) << (SECTIONS - 1 - level))
    return result


def frequency_order():
    series = jnp.arange(LEN, dtype=jnp.int32)
    blocks = series // TOK_DEV
    within = series % TOK_DEV
    return (N_CTX * within + reverse_digits(blocks)).astype(jnp.int32)


def reference(output_gradient, input_spectrum, filter_spectrum):
    frequency = frequency_order()
    filter_complex = filter_spectrum[:, 0] + 1j * filter_spectrum[:, 1]
    positions = jnp.arange(LEN, dtype=jnp.int32)
    twist = jnp.exp((-0.5j * jnp.pi / LEN) * positions)
    untwist = jnp.exp((0.5j * jnp.pi / LEN) * positions)

    def per_sequence(carry, inputs):
        samples, saved = inputs
        spectrum = jnp.fft.fft(samples * twist, axis=-1)[:, frequency]
        product = spectrum * jnp.conj(filter_complex)
        whole = jnp.zeros((CHANS, LEN), spectrum.dtype).at[:, frequency].set(product)
        gradient = jnp.real(jnp.fft.ifft(whole, axis=-1) * untwist)
        saved_complex = saved[:, 0] + 1j * saved[:, 1]
        term = spectrum * jnp.conj(saved_complex)
        totals = (carry[0] + jnp.real(term).astype(jnp.float32), carry[1] + jnp.imag(term).astype(jnp.float32))
        return totals, gradient.astype(jnp.float32)

    start = jnp.zeros((CHANS, LEN), jnp.float32)
    totals, input_gradient = lax.scan(per_sequence, (start, start), (output_gradient, input_spectrum))
    return input_gradient, jnp.stack([totals[0], totals[1]], axis=1)
```

```python
import functools
import math

import jax
import jax.numpy as jnp
import numpy as np
from jax import lax
from jax.experimental import pallas as pl
from jax.experimental.pallas import tpu as pltpu
from jax.sharding import PartitionSpec as P

INTERPRET = False
RANKS = 16
CHANS = 8
LANES = 128
ROWS = 64
TOKENS = ROWS * LANES
LENGTH = RANKS * TOKENS
SLICE = TOKENS // RANKS
TILES = SLICE // LANES

VMEM = pl.BlockSpec(memory_space=pltpu.VMEM)
SMEM = pl.BlockSpec(memory_space=pltpu.SMEM)


def reversed_digits(index, sections=4):
    return sum((index >> level & 1) << sections - 1 - level for level in range(sections))


def rotor(angle_over_circle):
    angle = 2.0 * math.pi * angle_over_circle
    return (math.cos(angle), math.sin(angle))


def times(value, factor):
    real, imag = value
    cosine, sine = factor
    return (real * cosine - imag * sine, real * sine + imag * cosine)


def plus(left, right):
    return (left[0] + right[0], left[1] + right[1])


def minus(left, right):
    return (left[0] - right[0], left[1] - right[1])


def quarter(value, sign):
    real, imag = value
    return (-imag, real) if sign > 0 else (imag, -real)


def dft4(values, sign):
    even_sum, even_diff = plus(values[0], values[2]), minus(values[0], values[2])
    odd_sum, odd_diff = plus(values[1], values[3]), minus(values[1], values[3])
    turned = quarter(odd_diff, sign)
    return [plus(even_sum, odd_sum), plus(even_diff, turned), minus(even_sum, odd_sum), minus(even_diff, turned)]


def dft8(values, sign):
    even = dft4(values[0::2], sign)
    odd = dft4(values[1::2], sign)
    half = math.sqrt(0.5)
    real, imag = odd[1]
    one = ((real - imag) * half, (real + imag) * half) if sign > 0 else ((real + imag) * half, (imag - real) * half)
    real, imag = odd[3]
    three = ((-real - imag) * half, (real - imag) * half) if sign > 0 else ((imag - real) * half, (-real - imag) * half)
    odd = [odd[0], one, quarter(odd[2], sign), three]
    return [plus(even[k], odd[k]) for k in range(4)] + [minus(even[k], odd[k]) for k in range(4)]


def spread_kernel(samples_ref, out_ref):
    for tile in range(TILES):
        lanes = slice(tile * LANES, (tile + 1) * LANES)
        first = []
        for low in range(4):
            turned = []
            for high in range(4):
                sample = samples_ref[4 * high + low, :, lanes]
                cosine, sine = rotor(-high / 16)
                turned.append((sample * cosine, sample * sine))
            turned[0] = (samples_ref[low, :, lanes], jnp.zeros((CHANS, LANES), jnp.float32))
            first.append(dft4(turned, -1))
        for residue in range(4):
            last = [first[0][residue]] + [
                times(first[low][residue], rotor(-(4 * residue + 1) * low / 64)) for low in range(1, 4)
            ]
            for high, (real, imag) in enumerate(dft4(last, -1)):
                owner = reversed_digits(4 * high + residue)
                out_ref[owner, 0, :, lanes] = real
                out_ref[owner, 1, :, lanes] = imag


def gather_kernel(parts_ref, out_ref):
    for tile in range(TILES):
        lanes = slice(tile * LANES, (tile + 1) * LANES)
        first = []
        for residue in range(4):
            owners = [reversed_digits(4 * high + residue) for high in range(4)]
            values = dft4([(parts_ref[o, 0, :, lanes], parts_ref[o, 1, :, lanes]) for o in owners], 1)
            first.append(
                [values[0]] + [times(values[low], rotor((4 * residue + 1) * low / 64)) for low in range(1, 4)]
            )
        for low in range(4):
            values = dft4([first[residue][low] for residue in range(4)], 1)
            for high in range(4):
                cosine, sine = rotor(high / 16)
                real, imag = values[high]
                out_ref[4 * high + low, :, lanes] = real if high == 0 else real * cosine - imag * sine


def product(rows, high_ref, low_ref):
    high = rows.astype(jnp.bfloat16)
    low = (rows - high.astype(jnp.float32)).astype(jnp.bfloat16)
    dot = functools.partial(jnp.dot, preferred_element_type=jnp.float32)
    return dot(high, high_ref[...]) + dot(low, high_ref[...]) + dot(high, low_ref[...])


def local_kernel(
    mixed_ref, filter_ref, scalars_ref, shift_ref, middle_ref, there_high, there_low, back_high, back_low,
    out_ref, spectrum_ref, work_ref, twiddle_ref,
):
    shift = (shift_ref[0:1, :], shift_ref[1:2, :])
    real, imag = times((middle_ref[0], middle_ref[1]), shift)
    twiddle_ref[0] = real
    twiddle_ref[1] = imag

    def scalar(index, sign):
        return (scalars_ref[index, 0], scalars_ref[index, 1] * sign)

    def row(index, sign):
        whole = (CHANS, LANES)
        real = jnp.broadcast_to(twiddle_ref[0, index : index + 1, :], whole)
        imag = jnp.broadcast_to(twiddle_ref[1, index : index + 1, :], whole)
        return (real, imag if sign > 0 else -imag)

    def source(index):
        lanes = slice(index % TILES * LANES, (index % TILES + 1) * LANES)
        return index // TILES, lanes

    for inner in range(8):
        values = []
        for outer in range(8):
            rank, lanes = source(8 * outer + inner)
            value = (mixed_ref[rank, 0, :, lanes], mixed_ref[rank, 1, :, lanes])
            values.append(times(value, scalar(outer, 1)) if outer else value)
        values = dft8(values, -1)
        for a in range(8):
            real, imag = times(values[a], scalar(8 + 8 * inner + a, 1)) if inner else values[a]
            work_ref[8 * inner + a, :, :LANES] = real
            work_ref[8 * inner + a, :, LANES:] = imag
    for a in range(8):
        values = dft8(
            [(work_ref[8 * inner + a, :, :LANES], work_ref[8 * inner + a, :, LANES:]) for inner in range(8)], -1
        )
        for b in range(8):
            real, imag = times(values[b], row(a + 8 * b, 1))
            work_ref[8 * b + a, :, :LANES] = real
            work_ref[8 * b + a, :, LANES:] = imag

    spectrum = product(work_ref[...].reshape(ROWS * CHANS, 2 * LANES), there_high, there_low)
    spectrum_ref[...] = spectrum.reshape(ROWS, CHANS, 2 * LANES)
    filters = filter_ref[...].reshape(ROWS * CHANS, 2 * LANES)
    real, imag = times(
        (spectrum[:, :LANES], spectrum[:, LANES:]), (filters[:, :LANES], -filters[:, LANES:])
    )
    back = product(jnp.concatenate([real, imag], axis=1), back_high, back_low)
    work_ref[...] = back.reshape(ROWS, CHANS, 2 * LANES)

    for a in range(8):
        values = []
        for b in range(8):
            value = (work_ref[8 * b + a, :, :LANES], work_ref[8 * b + a, :, LANES:])
            values.append(times(value, row(a + 8 * b, -1)))
        values = dft8(values, 1)
        for inner in range(8):
            real, imag = times(values[inner], scalar(8 + 8 * inner + a, -1)) if inner else values[inner]
            work_ref[8 * inner + a, :, :LANES] = real
            work_ref[8 * inner + a, :, LANES:] = imag
    for inner in range(8):
        values = dft8(
            [(work_ref[8 * inner + a, :, :LANES], work_ref[8 * inner + a, :, LANES:]) for a in range(8)], 1
        )
        for outer in range(8):
            real, imag = times(values[outer], scalar(outer, -1)) if outer else values[outer]
            rank, lanes = source(8 * outer + inner)
            out_ref[rank, 0, :, lanes] = real
            out_ref[rank, 1, :, lanes] = imag


def term_kernel(spectrum_ref, saved_ref, out_ref):
    owners, rows = out_ref.shape[0], out_ref.shape[1] // 2
    spectrum = spectrum_ref[...].reshape(ROWS * CHANS, 2 * LANES)
    saved = saved_ref[...].reshape(ROWS * CHANS, 2 * LANES)
    term = times((spectrum[:, :LANES], spectrum[:, LANES:]), (saved[:, :LANES], -saved[:, LANES:]))
    for part in range(2):
        turned = term[part].T
        for owner in range(owners):
            out_ref[owner, part * rows : (part + 1) * rows, :] = turned[owner * rows : (owner + 1) * rows, :]


def call(kernel, out_shapes, in_specs, scratch=()):
    outs = [jax.ShapeDtypeStruct(shape, jnp.float32) for shape in out_shapes]
    return pl.pallas_call(
        kernel,
        out_shape=outs if len(outs) > 1 else outs[0],
        in_specs=in_specs,
        out_specs=[VMEM] * len(outs) if len(outs) > 1 else VMEM,
        scratch_shapes=list(scratch),
        interpret=INTERPRET,
    )


def split_table(table):
    table = table.astype(np.float32)
    high = table.astype(jnp.bfloat16)
    low = (table - high.astype(np.float32)).astype(jnp.bfloat16)
    return high, low


def tables():
    lane = np.arange(LANES)
    angle = 2.0 * np.pi / LANES * (lane[:, None] * lane[None, :] % LANES)
    cosine, sine = np.cos(angle), np.sin(angle)
    there = np.block([[cosine, -sine], [sine, cosine]])
    back = np.block([[cosine, sine], [-sine, cosine]]) / LENGTH
    middle_angle = -2.0 * np.pi / TOKENS * (np.arange(ROWS)[:, None] * lane[None, :])
    middle = np.stack([np.cos(middle_angle), np.sin(middle_angle)]).astype(np.float32)
    scalars = np.zeros((RANKS, 72, 2), np.float32)
    shift = np.zeros((RANKS, 2, LANES), np.float32)
    series = np.arange(8)
    for rank in range(RANKS):
        step = 4 * reversed_digits(rank) + 1
        outer = -2.0 * np.pi * step * 8 * series / 4096
        inner = -2.0 * np.pi * (step * series[:, None] / 4096 + series[:, None] * series[None, :] / 64)
        angles = np.concatenate([outer, inner.reshape(-1)])
        scalars[rank] = np.stack([np.cos(angles), np.sin(angles)], axis=1)
        lanes = -2.0 * np.pi * step * lane / (4 * LENGTH)
        shift[rank] = np.stack([np.cos(lanes), np.sin(lanes)])
    return split_table(there), split_table(back), middle, scalars, shift


def by_frequency(spectrum):
    parts = spectrum.reshape(CHANS, 2, LANES, ROWS)
    return jnp.transpose(parts, (3, 0, 1, 2)).reshape(ROWS, CHANS, 2 * LANES)


def per_device(output_gradient, input_spectrum, filter_spectrum):
    owners = lax.axis_size("dp")
    rank = lax.axis_index("ctx")
    there, back, middle, scalars, shift = tables()
    own = lambda table: lax.dynamic_index_in_dim(jnp.asarray(table), rank, 0, keepdims=False)
    exchange = lambda array, axis: lax.all_to_all(array, axis, split_axis=0, concat_axis=0, tiled=True)

    slices = jnp.transpose(output_gradient.reshape(CHANS, RANKS, SLICE), (1, 0, 2))
    samples = exchange(slices, "ctx")
    filters = by_frequency(filter_spectrum)
    saved = by_frequency(input_spectrum[0])
    mixed = call(spread_kernel, [(RANKS, 2, CHANS, SLICE)], [VMEM])(samples)
    mixed = exchange(mixed, "ctx")
    work = (ROWS, CHANS, 2 * LANES)
    parts, spectrum = call(
        local_kernel,
        [(RANKS, 2, CHANS, SLICE), work],
        [VMEM, VMEM, SMEM] + [VMEM] * 6,
        [pltpu.VMEM(work, jnp.float32), pltpu.VMEM((2, ROWS, LANES), jnp.float32)],
    )(mixed, filters, own(scalars), own(shift), middle, *there, *back)
    parts = exchange(parts, "ctx")
    term = call(term_kernel, [(owners, 2 * LANES // owners, ROWS * CHANS)], [VMEM, VMEM])(spectrum, saved)
    blocks = call(gather_kernel, [(RANKS, CHANS, SLICE)], [VMEM])(parts)
    blocks = exchange(blocks, "ctx")
    input_gradient = jnp.transpose(blocks, (1, 0, 2)).reshape(1, CHANS, TOKENS)

    total = jnp.sum(exchange(term, "dp"), axis=0)
    total = total.reshape(2, LANES // owners, ROWS, CHANS)
    filter_gradient = jnp.transpose(total, (3, 0, 1, 2)).reshape(CHANS, 2, TOKENS // owners)
    return (input_gradient, filter_gradient)


def solution(mesh):
    in_specs = (P("dp", None, "ctx"), P("dp", None, None, "ctx"), P(None, None, "ctx"))
    out_specs = (P("dp", None, "ctx"), P(None, None, ("ctx", "dp")))
    return jax.shard_map(
        per_device, mesh=mesh, in_specs=in_specs, out_specs=out_specs, check_vma=False
    )
```

```python
import functools
import math

import jax
import jax.numpy as jnp
import numpy as np
from jax import lax
from jax.experimental import pallas as pl
from jax.experimental.pallas import tpu as pltpu
from jax.sharding import PartitionSpec as P

INTERPRET = False
RANKS = 16
CHANS = 8
LANES = 128
ROWS = 64
TOKENS = ROWS * LANES
LENGTH = RANKS * TOKENS
SLICE = TOKENS // RANKS
TILES = SLICE // LANES

VMEM = pl.BlockSpec(memory_space=pltpu.VMEM)
SMEM = pl.BlockSpec(memory_space=pltpu.SMEM)


def reversed_digits(index, sections=4):
    return sum((index >> level & 1) << sections - 1 - level for level in range(sections))


def rotor(angle_over_circle):
    angle = 2.0 * math.pi * angle_over_circle
    return (math.cos(angle), math.sin(angle))


def times(value, factor):
    real, imag = value
    cosine, sine = factor
    return (real * cosine - imag * sine, real * sine + imag * cosine)


def plus(left, right):
    return (left[0] + right[0], left[1] + right[1])


def minus(left, right):
    return (left[0] - right[0], left[1] - right[1])


def quarter(value, sign):
    real, imag = value
    return (-imag, real) if sign > 0 else (imag, -real)


def dft4(values, sign):
    even_sum, even_diff = plus(values[0], values[2]), minus(values[0], values[2])
    odd_sum, odd_diff = plus(values[1], values[3]), minus(values[1], values[3])
    turned = quarter(odd_diff, sign)
    return [plus(even_sum, odd_sum), plus(even_diff, turned), minus(even_sum, odd_sum), minus(even_diff, turned)]


def dft8(values, sign):
    even = dft4(values[0::2], sign)
    odd = dft4(values[1::2], sign)
    half = math.sqrt(0.5)
    real, imag = odd[1]
    one = ((real - imag) * half, (real + imag) * half) if sign > 0 else ((real + imag) * half, (imag - real) * half)
    real, imag = odd[3]
    three = ((-real - imag) * half, (real - imag) * half) if sign > 0 else ((imag - real) * half, (-real - imag) * half)
    odd = [odd[0], one, quarter(odd[2], sign), three]
    return [plus(even[k], odd[k]) for k in range(4)] + [minus(even[k], odd[k]) for k in range(4)]


def spread_kernel(samples_ref, out_ref):
    for tile in range(TILES):
        lanes = slice(tile * LANES, (tile + 1) * LANES)
        first = []
        for low in range(4):
            turned = []
            for high in range(4):
                sample = samples_ref[4 * high + low, :, lanes]
                cosine, sine = rotor(-high / 16)
                turned.append((sample * cosine, sample * sine))
            turned[0] = (samples_ref[low, :, lanes], jnp.zeros((CHANS, LANES), jnp.float32))
            first.append(dft4(turned, -1))
        for residue in range(4):
            last = [first[0][residue]] + [
                times(first[low][residue], rotor(-(4 * residue + 1) * low / 64)) for low in range(1, 4)
            ]
            for high, (real, imag) in enumerate(dft4(last, -1)):
                owner = reversed_digits(4 * high + residue)
                out_ref[owner, 0, :, lanes] = real
                out_ref[owner, 1, :, lanes] = imag


def gather_kernel(parts_ref, out_ref):
    for tile in range(TILES):
        lanes = slice(tile * LANES, (tile + 1) * LANES)
        first = []
        for residue in range(4):
            owners = [reversed_digits(4 * high + residue) for high in range(4)]
            values = dft4([(parts_ref[o, 0, :, lanes], parts_ref[o, 1, :, lanes]) for o in owners], 1)
            first.append(
                [values[0]] + [times(values[low], rotor((4 * residue + 1) * low / 64)) for low in range(1, 4)]
            )
        for low in range(4):
            values = dft4([first[residue][low] for residue in range(4)], 1)
            for high in range(4):
                cosine, sine = rotor(high / 16)
                real, imag = values[high]
                out_ref[4 * high + low, :, lanes] = real if high == 0 else real * cosine - imag * sine


def product(rows, high_ref, low_ref):
    high = rows.astype(jnp.bfloat16)
    low = (rows - high.astype(jnp.float32)).astype(jnp.bfloat16)
    dot = functools.partial(jnp.dot, preferred_element_type=jnp.float32)
    return dot(high, high_ref[...]) + dot(low, high_ref[...]) + dot(high, low_ref[...])


def local_kernel(
    mixed_ref, filter_ref, scalars_ref, shift_ref, middle_ref, there_high, there_low, back_high, back_low,
    out_ref, spectrum_ref, work_ref, twiddle_ref,
):
    shift = (shift_ref[0:1, :], shift_ref[1:2, :])
    real, imag = times((middle_ref[0], middle_ref[1]), shift)
    twiddle_ref[0] = real
    twiddle_ref[1] = imag

    def scalar(index, sign):
        return (scalars_ref[index, 0], scalars_ref[index, 1] * sign)

    def row(index, sign):
        whole = (CHANS, LANES)
        real = jnp.broadcast_to(twiddle_ref[0, index : index + 1, :], whole)
        imag = jnp.broadcast_to(twiddle_ref[1, index : index + 1, :], whole)
        return (real, imag if sign > 0 else -imag)

    def source(index):
        lanes = slice(index % TILES * LANES, (index % TILES + 1) * LANES)
        return index // TILES, lanes

    for inner in range(8):
        values = []
        for outer in range(8):
            rank, lanes = source(8 * outer + inner)
            value = (mixed_ref[rank, 0, :, lanes], mixed_ref[rank, 1, :, lanes])
            values.append(times(value, scalar(outer, 1)) if outer else value)
        values = dft8(values, -1)
        for a in range(8):
            real, imag = times(values[a], scalar(8 + 8 * inner + a, 1)) if inner else values[a]
            work_ref[8 * inner + a, :, :LANES] = real
            work_ref[8 * inner + a, :, LANES:] = imag
    for a in range(8):
        values = dft8(
            [(work_ref[8 * inner + a, :, :LANES], work_ref[8 * inner + a, :, LANES:]) for inner in range(8)], -1
        )
        for b in range(8):
            real, imag = times(values[b], row(a + 8 * b, 1))
            work_ref[8 * b + a, :, :LANES] = real
            work_ref[8 * b + a, :, LANES:] = imag

    spectrum = product(work_ref[...].reshape(ROWS * CHANS, 2 * LANES), there_high, there_low)
    spectrum_ref[...] = spectrum.reshape(ROWS, CHANS, 2 * LANES)
    filters = filter_ref[...].reshape(ROWS * CHANS, 2 * LANES)
    real, imag = times(
        (spectrum[:, :LANES], spectrum[:, LANES:]), (filters[:, :LANES], -filters[:, LANES:])
    )
    back = product(jnp.concatenate([real, imag], axis=1), back_high, back_low)
    work_ref[...] = back.reshape(ROWS, CHANS, 2 * LANES)

    for a in range(8):
        values = []
        for b in range(8):
            value = (work_ref[8 * b + a, :, :LANES], work_ref[8 * b + a, :, LANES:])
            values.append(times(value, row(a + 8 * b, -1)))
        values = dft8(values, 1)
        for inner in range(8):
            real, imag = times(values[inner], scalar(8 + 8 * inner + a, -1)) if inner else values[inner]
            work_ref[8 * inner + a, :, :LANES] = real
            work_ref[8 * inner + a, :, LANES:] = imag
    for inner in range(8):
        values = dft8(
            [(work_ref[8 * inner + a, :, :LANES], work_ref[8 * inner + a, :, LANES:]) for a in range(8)], 1
        )
        for outer in range(8):
            real, imag = times(values[outer], scalar(outer, -1)) if outer else values[outer]
            rank, lanes = source(8 * outer + inner)
            out_ref[rank, 0, :, lanes] = real
            out_ref[rank, 1, :, lanes] = imag


def term_kernel(rank_ref, spectrum_ref, saved_ref, keep_ref, send_ref):
    owners, rows = 2 * keep_ref.shape[0], keep_ref.shape[1] // 2
    rank = rank_ref[0]
    spectrum = spectrum_ref[...].reshape(ROWS * CHANS, 2 * LANES)
    saved = saved_ref[...].reshape(ROWS * CHANS, 2 * LANES)
    term = times((spectrum[:, :LANES], spectrum[:, LANES:]), (saved[:, :LANES], -saved[:, LANES:]))
    turned = [part.T for part in term]
    for pair in range(owners // 2):
        apart = rank >> 1 ^ pair
        slot = (apart & 3) << 2 | apart >> 2
        for part in range(2):
            place = slice(part * rows, (part + 1) * rows)
            even = turned[part][2 * pair * rows : (2 * pair + 1) * rows, :]
            odd = turned[part][(2 * pair + 1) * rows : (2 * pair + 2) * rows, :]
            keep_ref[slot, place, :] = jnp.where(rank & 1 == 0, even, odd)
            send_ref[slot, place, :] = jnp.where(rank & 1 == 0, odd, even)


def summed(total, sent):
    for array in sent:
        total = total + array
    return total


def sum_over_sequences(keep, send, owners):
    def swap(array, apart):
        return lax.ppermute(array, "dp", [(i, i ^ apart) for i in range(owners)])

    total = keep + swap(send, 1)
    total = total.reshape(4, 4, *keep.shape[1:])
    total = summed(total[0], [swap(total[k], k << 1) for k in range(1, 4)])
    return summed(total[0], [swap(total[k], k << 3) for k in range(1, 4)])


def call(kernel, outs, in_specs, scratch=()):
    specs = [pl.BlockSpec(memory_space=out.memory_space) for out in outs]
    return pl.pallas_call(
        kernel,
        out_shape=outs if len(outs) > 1 else outs[0],
        in_specs=in_specs,
        out_specs=specs if len(specs) > 1 else specs[0],
        scratch_shapes=list(scratch),
        interpret=INTERPRET,
    )


def on_chip(array):
    return array if INTERPRET else pltpu.with_memory_space_constraint(array, pltpu.VMEM)


def split_table(table):
    table = table.astype(np.float32)
    high = table.astype(jnp.bfloat16)
    low = (table - high.astype(np.float32)).astype(jnp.bfloat16)
    return high, low


def tables():
    lane = np.arange(LANES)
    angle = 2.0 * np.pi / LANES * (lane[:, None] * lane[None, :] % LANES)
    cosine, sine = np.cos(angle), np.sin(angle)
    there = np.block([[cosine, -sine], [sine, cosine]])
    back = np.block([[cosine, sine], [-sine, cosine]]) / LENGTH
    middle_angle = -2.0 * np.pi / TOKENS * (np.arange(ROWS)[:, None] * lane[None, :])
    middle = np.stack([np.cos(middle_angle), np.sin(middle_angle)]).astype(np.float32)
    scalars = np.zeros((RANKS, 72, 2), np.float32)
    shift = np.zeros((RANKS, 2, LANES), np.float32)
    series = np.arange(8)
    for rank in range(RANKS):
        step = 4 * reversed_digits(rank) + 1
        outer = -2.0 * np.pi * step * 8 * series / 4096
        inner = -2.0 * np.pi * (step * series[:, None] / 4096 + series[:, None] * series[None, :] / 64)
        angles = np.concatenate([outer, inner.reshape(-1)])
        scalars[rank] = np.stack([np.cos(angles), np.sin(angles)], axis=1)
        lanes = -2.0 * np.pi * step * lane / (4 * LENGTH)
        shift[rank] = np.stack([np.cos(lanes), np.sin(lanes)])
    return split_table(there), split_table(back), middle, scalars, shift


def by_frequency(spectrum):
    parts = spectrum.reshape(CHANS, 2, LANES, ROWS)
    return jnp.transpose(parts, (3, 0, 1, 2)).reshape(ROWS, CHANS, 2 * LANES)


def per_device(output_gradient, input_spectrum, filter_spectrum):
    owners = lax.axis_size("dp")
    rank = lax.axis_index("ctx")
    there, back, middle, scalars, shift = tables()
    own = lambda table: lax.dynamic_index_in_dim(jnp.asarray(table), rank, 0, keepdims=False)
    exchange = lambda array, axis: lax.all_to_all(array, axis, split_axis=0, concat_axis=0, tiled=True)

    slices = jnp.transpose(output_gradient.reshape(CHANS, RANKS, SLICE), (1, 0, 2))
    samples = exchange(slices, "ctx")
    filters = by_frequency(filter_spectrum)
    saved = by_frequency(input_spectrum[0])
    mixed = call(spread_kernel, [pltpu.VMEM((RANKS, 2, CHANS, SLICE), jnp.float32)], [VMEM])(on_chip(samples))
    mixed = exchange(mixed, "ctx")
    work = (ROWS, CHANS, 2 * LANES)
    parts, spectrum = call(
        local_kernel,
        [pltpu.VMEM((RANKS, 2, CHANS, SLICE), jnp.float32), pltpu.VMEM(work, jnp.float32)],
        [VMEM, VMEM, SMEM] + [VMEM] * 6,
        [pltpu.VMEM(work, jnp.float32), pltpu.VMEM((2, ROWS, LANES), jnp.float32)],
    )(on_chip(mixed), on_chip(filters), own(scalars), own(shift), middle, *there, *back)
    parts = exchange(parts, "ctx")
    half = pltpu.VMEM((owners // 2, 2 * LANES // owners, ROWS * CHANS), jnp.float32)
    keep, send = call(term_kernel, [half, half], [SMEM, VMEM, VMEM])(
        lax.axis_index("dp").reshape(1), on_chip(spectrum), on_chip(saved)
    )
    total = sum_over_sequences(keep, send, owners)
    blocks = call(gather_kernel, [pltpu.VMEM((RANKS, CHANS, SLICE), jnp.float32)], [VMEM])(on_chip(parts))
    blocks = exchange(blocks, "ctx")
    input_gradient = jnp.transpose(blocks, (1, 0, 2)).reshape(1, CHANS, TOKENS)
    total = total.reshape(2, LANES // owners, ROWS, CHANS)
    filter_gradient = jnp.transpose(total, (3, 0, 1, 2)).reshape(CHANS, 2, TOKENS // owners)
    return (input_gradient, filter_gradient)


def solution(mesh):
    in_specs = (P("dp", None, "ctx"), P("dp", None, None, "ctx"), P(None, None, "ctx"))
    out_specs = (P("dp", None, "ctx"), P(None, None, ("ctx", "dp")))
    return jax.shard_map(
        per_device, mesh=mesh, in_specs=in_specs, out_specs=out_specs, check_vma=False
    )
```

```python
import functools
import math

import jax
import jax.numpy as jnp
import numpy as np
from jax import lax
from jax.experimental import pallas as pl
from jax.experimental.pallas import tpu as pltpu
from jax.sharding import PartitionSpec as P

INTERPRET = False
RANKS = 16
CHANS = 8
LANES = 128
ROWS = 64
TOKENS = ROWS * LANES
LENGTH = RANKS * TOKENS
SLICE = TOKENS // RANKS
TILES = SLICE // LANES

VMEM = pl.BlockSpec(memory_space=pltpu.VMEM)
SMEM = pl.BlockSpec(memory_space=pltpu.SMEM)


def reversed_digits(index, sections=4):
    return sum((index >> level & 1) << sections - 1 - level for level in range(sections))


def rotor(angle_over_circle):
    angle = 2.0 * math.pi * angle_over_circle
    return (math.cos(angle), math.sin(angle))


def times(value, factor):
    real, imag = value
    cosine, sine = factor
    return (real * cosine - imag * sine, real * sine + imag * cosine)


def plus(left, right):
    return (left[0] + right[0], left[1] + right[1])


def minus(left, right):
    return (left[0] - right[0], left[1] - right[1])


def quarter(value, sign):
    real, imag = value
    return (-imag, real) if sign > 0 else (imag, -real)


def dft4(values, sign):
    even_sum, even_diff = plus(values[0], values[2]), minus(values[0], values[2])
    odd_sum, odd_diff = plus(values[1], values[3]), minus(values[1], values[3])
    turned = quarter(odd_diff, sign)
    return [plus(even_sum, odd_sum), plus(even_diff, turned), minus(even_sum, odd_sum), minus(even_diff, turned)]


def dft8(values, sign):
    even = dft4(values[0::2], sign)
    odd = dft4(values[1::2], sign)
    half = math.sqrt(0.5)
    real, imag = odd[1]
    one = ((real - imag) * half, (real + imag) * half) if sign > 0 else ((real + imag) * half, (imag - real) * half)
    real, imag = odd[3]
    three = ((-real - imag) * half, (real - imag) * half) if sign > 0 else ((imag - real) * half, (-real - imag) * half)
    odd = [odd[0], one, quarter(odd[2], sign), three]
    return [plus(even[k], odd[k]) for k in range(4)] + [minus(even[k], odd[k]) for k in range(4)]


def spread_kernel(samples_ref, out_ref):
    for tile in range(TILES):
        lanes = slice(tile * LANES, (tile + 1) * LANES)
        first = []
        for low in range(4):
            turned = []
            for high in range(4):
                sample = samples_ref[4 * high + low, :, lanes]
                cosine, sine = rotor(-high / 16)
                turned.append((sample * cosine, sample * sine))
            turned[0] = (samples_ref[low, :, lanes], jnp.zeros((CHANS, LANES), jnp.float32))
            first.append(dft4(turned, -1))
        for residue in range(4):
            last = [first[0][residue]] + [
                times(first[low][residue], rotor(-(4 * residue + 1) * low / 64)) for low in range(1, 4)
            ]
            for high, (real, imag) in enumerate(dft4(last, -1)):
                owner = reversed_digits(4 * high + residue)
                out_ref[owner, 0, :, lanes] = real
                out_ref[owner, 1, :, lanes] = imag


def gather_kernel(parts_ref, out_ref):
    for tile in range(TILES):
        lanes = slice(tile * LANES, (tile + 1) * LANES)
        first = []
        for residue in range(4):
            owners = [reversed_digits(4 * high + residue) for high in range(4)]
            values = dft4([(parts_ref[o, 0, :, lanes], parts_ref[o, 1, :, lanes]) for o in owners], 1)
            first.append(
                [values[0]] + [times(values[low], rotor((4 * residue + 1) * low / 64)) for low in range(1, 4)]
            )
        for low in range(4):
            values = dft4([first[residue][low] for residue in range(4)], 1)
            for high in range(4):
                cosine, sine = rotor(high / 16)
                real, imag = values[high]
                out_ref[4 * high + low, :, lanes] = real if high == 0 else real * cosine - imag * sine


def product(rows, high_ref, low_ref):
    high = rows.astype(jnp.bfloat16)
    low = (rows - high.astype(jnp.float32)).astype(jnp.bfloat16)
    dot = functools.partial(jnp.dot, preferred_element_type=jnp.float32)
    return dot(high, high_ref[...]) + dot(low, high_ref[...]) + dot(high, low_ref[...])


def twiddles(shift_ref, middle_ref, twiddle_ref):
    shift = (shift_ref[0:1, :], shift_ref[1:2, :])
    twiddle_ref[0], twiddle_ref[1] = times((middle_ref[0], middle_ref[1]), shift)


def twiddle_row(twiddle_ref, index, sign):
    whole = (CHANS, LANES)
    real = jnp.broadcast_to(twiddle_ref[0, index : index + 1, :], whole)
    imag = jnp.broadcast_to(twiddle_ref[1, index : index + 1, :], whole)
    return (real, imag if sign > 0 else -imag)


def source(index):
    lanes = slice(index % TILES * LANES, (index % TILES + 1) * LANES)
    return index // TILES, lanes


def load(ref, index):
    return (ref[index, :, :LANES], ref[index, :, LANES:])


def store(ref, index, value):
    ref[index, :, :LANES], ref[index, :, LANES:] = value


def forward_kernel(
    mixed_ref, scalars_ref, shift_ref, middle_ref, high_ref, low_ref, spectrum_ref, work_ref, twiddle_ref
):
    twiddles(shift_ref, middle_ref, twiddle_ref)

    def scalar(index):
        return twiddle_row(scalars_ref, index, 1)

    for inner in range(8):
        values = []
        for outer in range(8):
            rank, lanes = source(8 * outer + inner)
            value = (mixed_ref[rank, 0, :, lanes], mixed_ref[rank, 1, :, lanes])
            values.append(times(value, scalar(outer)) if outer else value)
        values = dft8(values, -1)
        for a in range(8):
            store(work_ref, 8 * inner + a, times(values[a], scalar(8 + 8 * inner + a)) if inner else values[a])
    for a in range(8):
        values = dft8([load(work_ref, 8 * inner + a) for inner in range(8)], -1)
        for b in range(8):
            store(work_ref, 8 * b + a, times(values[b], twiddle_row(twiddle_ref, a + 8 * b, 1)))
    spectrum = product(work_ref[...].reshape(ROWS * CHANS, 2 * LANES), high_ref, low_ref)
    spectrum_ref[...] = spectrum.reshape(ROWS, CHANS, 2 * LANES)


def inverse_kernel(
    spectrum_ref, filter_ref, scalars_ref, shift_ref, middle_ref, high_ref, low_ref, out_ref, work_ref, twiddle_ref
):
    twiddles(shift_ref, middle_ref, twiddle_ref)

    def scalar(index):
        return twiddle_row(scalars_ref, index, -1)

    spectrum = spectrum_ref[...].reshape(ROWS * CHANS, 2 * LANES)
    filters = filter_ref[...].reshape(ROWS * CHANS, 2 * LANES)
    real, imag = times((spectrum[:, :LANES], spectrum[:, LANES:]), (filters[:, :LANES], -filters[:, LANES:]))
    back = product(jnp.concatenate([real, imag], axis=1), high_ref, low_ref)
    work_ref[...] = back.reshape(ROWS, CHANS, 2 * LANES)
    for a in range(8):
        values = []
        for b in range(8):
            values.append(times(load(work_ref, 8 * b + a), twiddle_row(twiddle_ref, a + 8 * b, -1)))
        values = dft8(values, 1)
        for inner in range(8):
            value = values[inner]
            store(work_ref, 8 * inner + a, times(value, scalar(8 + 8 * inner + a)) if inner else value)
    for inner in range(8):
        values = dft8([load(work_ref, 8 * inner + a) for a in range(8)], 1)
        for outer in range(8):
            real, imag = times(values[outer], scalar(outer)) if outer else values[outer]
            rank, lanes = source(8 * outer + inner)
            out_ref[rank, 0, :, lanes] = real
            out_ref[rank, 1, :, lanes] = imag


def term_kernel(rank_ref, spectrum_ref, saved_ref, keep_ref, send_ref):
    owners, rows = 2 * keep_ref.shape[0], keep_ref.shape[1] // 2
    rank = rank_ref[0]
    spectrum = spectrum_ref[...].reshape(ROWS * CHANS, 2 * LANES)
    saved = saved_ref[...].reshape(ROWS * CHANS, 2 * LANES)
    term = times((spectrum[:, :LANES], spectrum[:, LANES:]), (saved[:, :LANES], -saved[:, LANES:]))
    turned = [part.T for part in term]
    for pair in range(owners // 2):
        apart = rank >> 1 ^ pair
        slot = (apart & 3) << 2 | apart >> 2
        for part in range(2):
            place = slice(part * rows, (part + 1) * rows)
            even = turned[part][2 * pair * rows : (2 * pair + 1) * rows, :]
            odd = turned[part][(2 * pair + 1) * rows : (2 * pair + 2) * rows, :]
            keep_ref[slot, place, :] = jnp.where(rank & 1 == 0, even, odd)
            send_ref[slot, place, :] = jnp.where(rank & 1 == 0, odd, even)


def summed(total, sent):
    for array in sent:
        total = total + array
    return total


def sum_over_sequences(keep, send, owners):
    def swap(array, apart):
        return lax.ppermute(array, "dp", [(i, i ^ apart) for i in range(owners)])

    total = keep + swap(send, 1)
    total = total.reshape(4, 4, *keep.shape[1:])
    total = summed(total[0], [swap(total[k], k << 1) for k in range(1, 4)])
    return summed(total[0], [swap(total[k], k << 3) for k in range(1, 4)])


def call(kernel, outs, in_specs, scratch=()):
    specs = [pl.BlockSpec(memory_space=out.memory_space) for out in outs]
    return pl.pallas_call(
        kernel,
        out_shape=outs if len(outs) > 1 else outs[0],
        in_specs=in_specs,
        out_specs=specs if len(specs) > 1 else specs[0],
        scratch_shapes=list(scratch),
        interpret=INTERPRET,
    )


def on_chip(array):
    return array if INTERPRET else pltpu.with_memory_space_constraint(array, pltpu.VMEM)


def split_table(table):
    table = table.astype(np.float32)
    high = table.astype(jnp.bfloat16)
    low = (table - high.astype(np.float32)).astype(jnp.bfloat16)
    return high, low


def tables():
    lane = np.arange(LANES)
    angle = 2.0 * np.pi / LANES * (lane[:, None] * lane[None, :] % LANES)
    cosine, sine = np.cos(angle), np.sin(angle)
    there = np.block([[cosine, -sine], [sine, cosine]])
    back = np.block([[cosine, sine], [-sine, cosine]]) / LENGTH
    middle_angle = -2.0 * np.pi / TOKENS * (np.arange(ROWS)[:, None] * lane[None, :])
    middle = np.stack([np.cos(middle_angle), np.sin(middle_angle)]).astype(np.float32)
    scalars = np.zeros((RANKS, 72, 2), np.float32)
    shift = np.zeros((RANKS, 2, LANES), np.float32)
    series = np.arange(8)
    for rank in range(RANKS):
        step = 4 * reversed_digits(rank) + 1
        outer = -2.0 * np.pi * step * 8 * series / 4096
        inner = -2.0 * np.pi * (step * series[:, None] / 4096 + series[:, None] * series[None, :] / 64)
        angles = np.concatenate([outer, inner.reshape(-1)])
        scalars[rank] = np.stack([np.cos(angles), np.sin(angles)], axis=1)
        lanes = -2.0 * np.pi * step * lane / (4 * LENGTH)
        shift[rank] = np.stack([np.cos(lanes), np.sin(lanes)])
    return split_table(there), split_table(back), middle, scalars, shift


def by_frequency(spectrum):
    parts = spectrum.reshape(CHANS, 2, LANES, ROWS)
    return jnp.transpose(parts, (3, 0, 1, 2)).reshape(ROWS, CHANS, 2 * LANES)


def per_device(output_gradient, input_spectrum, filter_spectrum):
    owners = lax.axis_size("dp")
    rank = lax.axis_index("ctx")
    there, back, middle, scalars, shift = tables()
    own = lambda table: lax.dynamic_index_in_dim(jnp.asarray(table), rank, 0, keepdims=False)
    exchange = lambda array, axis: lax.all_to_all(array, axis, split_axis=0, concat_axis=0, tiled=True)

    slices = jnp.transpose(output_gradient.reshape(CHANS, RANKS, SLICE), (1, 0, 2))
    samples = exchange(slices, "ctx")
    filters = by_frequency(filter_spectrum)
    saved = by_frequency(input_spectrum[0])
    mixed = call(spread_kernel, [pltpu.VMEM((RANKS, 2, CHANS, SLICE), jnp.float32)], [VMEM])(on_chip(samples))
    mixed = exchange(mixed, "ctx")
    work = (ROWS, CHANS, 2 * LANES)
    scratch = [pltpu.VMEM(work, jnp.float32), pltpu.VMEM((2, ROWS, LANES), jnp.float32)]
    scalars = on_chip(jnp.broadcast_to(own(scalars).T[:, :, None], (2, 72, LANES)))
    shift = on_chip(own(shift))
    middle = on_chip(jnp.asarray(middle))
    there, back = ([on_chip(jnp.asarray(table)) for table in pair] for pair in (there, back))
    spectrum = call(
        forward_kernel, [pltpu.VMEM(work, jnp.float32)], [VMEM] * 6, scratch
    )(on_chip(mixed), scalars, shift, middle, *there)
    half = pltpu.VMEM((owners // 2, 2 * LANES // owners, ROWS * CHANS), jnp.float32)
    keep, send = call(term_kernel, [half, half], [SMEM, VMEM, VMEM])(
        lax.axis_index("dp").reshape(1), on_chip(spectrum), on_chip(saved)
    )
    total = sum_over_sequences(keep, send, owners)
    parts = call(
        inverse_kernel,
        [pltpu.VMEM((RANKS, 2, CHANS, SLICE), jnp.float32)],
        [VMEM] * 7,
        scratch,
    )(on_chip(spectrum), on_chip(filters), scalars, shift, middle, *back)
    parts = exchange(parts, "ctx")
    blocks = call(gather_kernel, [pltpu.VMEM((RANKS, CHANS, SLICE), jnp.float32)], [VMEM])(on_chip(parts))
    blocks = exchange(blocks, "ctx")
    input_gradient = jnp.transpose(blocks, (1, 0, 2)).reshape(1, CHANS, TOKENS)
    total = total.reshape(2, LANES // owners, ROWS, CHANS)
    filter_gradient = jnp.transpose(total, (3, 0, 1, 2)).reshape(CHANS, 2, TOKENS // owners)
    return (input_gradient, filter_gradient)


def solution(mesh):
    in_specs = (P("dp", None, "ctx"), P("dp", None, None, "ctx"), P(None, None, "ctx"))
    out_specs = (P("dp", None, "ctx"), P(None, None, ("ctx", "dp")))
    return jax.shard_map(
        per_device, mesh=mesh, in_specs=in_specs, out_specs=out_specs, check_vma=False
    )
```

```python
import functools
import math

import jax
import jax.numpy as jnp
import numpy as np
from jax import lax
from jax.experimental import pallas as pl
from jax.experimental.pallas import tpu as pltpu
from jax.sharding import PartitionSpec as P

INTERPRET = False
RANKS = 16
CHANS = 8
LANES = 128
ROWS = 64
TOKENS = ROWS * LANES
LENGTH = RANKS * TOKENS
SLICE = TOKENS // RANKS
TILES = SLICE // LANES

VMEM = pl.BlockSpec(memory_space=pltpu.VMEM)
SMEM = pl.BlockSpec(memory_space=pltpu.SMEM)


def reversed_digits(index, sections=4):
    return sum((index >> level & 1) << sections - 1 - level for level in range(sections))


def rotor(angle_over_circle):
    angle = 2.0 * math.pi * angle_over_circle
    return (math.cos(angle), math.sin(angle))


def times(value, factor):
    real, imag = value
    cosine, sine = factor
    return (real * cosine - imag * sine, real * sine + imag * cosine)


def plus(left, right):
    return (left[0] + right[0], left[1] + right[1])


def minus(left, right):
    return (left[0] - right[0], left[1] - right[1])


def quarter(value, sign):
    real, imag = value
    return (-imag, real) if sign > 0 else (imag, -real)


def dft4(values, sign):
    even_sum, even_diff = plus(values[0], values[2]), minus(values[0], values[2])
    odd_sum, odd_diff = plus(values[1], values[3]), minus(values[1], values[3])
    turned = quarter(odd_diff, sign)
    return [plus(even_sum, odd_sum), plus(even_diff, turned), minus(even_sum, odd_sum), minus(even_diff, turned)]


def dft8(values, sign):
    even = dft4(values[0::2], sign)
    odd = dft4(values[1::2], sign)
    half = math.sqrt(0.5)
    real, imag = odd[1]
    one = ((real - imag) * half, (real + imag) * half) if sign > 0 else ((real + imag) * half, (imag - real) * half)
    real, imag = odd[3]
    three = ((-real - imag) * half, (real - imag) * half) if sign > 0 else ((imag - real) * half, (-real - imag) * half)
    odd = [odd[0], one, quarter(odd[2], sign), three]
    return [plus(even[k], odd[k]) for k in range(4)] + [minus(even[k], odd[k]) for k in range(4)]


def spread_kernel(samples_ref, sent_ref, out_ref, semaphores):
    copies = []
    for tile in range(TILES):
        lanes = slice(tile * LANES, (tile + 1) * LANES)
        first = []
        for low in range(4):
            turned = []
            for high in range(4):
                sample = samples_ref[4 * high + low, :, lanes]
                cosine, sine = rotor(-high / 16)
                turned.append((sample * cosine, sample * sine))
            turned[0] = (samples_ref[low, :, lanes], jnp.zeros((CHANS, LANES), jnp.float32))
            first.append(dft4(turned, -1))
        for residue in range(4):
            last = [first[0][residue]] + [
                times(first[low][residue], rotor(-(4 * residue + 1) * low / 64)) for low in range(1, 4)
            ]
            for high, (real, imag) in enumerate(dft4(last, -1)):
                owner = reversed_digits(4 * high + residue)
                out_ref[owner, 0, :, lanes] = real
                out_ref[owner, 1, :, lanes] = imag
        where = (slice(None), slice(None), slice(None), lanes)
        copies.append(pltpu.make_async_copy(out_ref.at[where], sent_ref.at[where], semaphores.at[tile]))
        copies[-1].start()
    for copy in copies:
        copy.wait()


def gather_kernel(parts_ref, sent_ref, out_ref, semaphores):
    copies = []
    for tile in range(TILES):
        lanes = slice(tile * LANES, (tile + 1) * LANES)
        first = []
        for residue in range(4):
            owners = [reversed_digits(4 * high + residue) for high in range(4)]
            values = dft4([(parts_ref[o, 0, :, lanes], parts_ref[o, 1, :, lanes]) for o in owners], 1)
            first.append(
                [values[0]] + [times(values[low], rotor((4 * residue + 1) * low / 64)) for low in range(1, 4)]
            )
        for low in range(4):
            values = dft4([first[residue][low] for residue in range(4)], 1)
            for high in range(4):
                cosine, sine = rotor(high / 16)
                real, imag = values[high]
                out_ref[4 * high + low, :, lanes] = real if high == 0 else real * cosine - imag * sine
        where = (slice(None), slice(None), lanes)
        copies.append(pltpu.make_async_copy(out_ref.at[where], sent_ref.at[where], semaphores.at[tile]))
        copies[-1].start()
    for copy in copies:
        copy.wait()


def product(rows, high_ref, low_ref):
    high = rows.astype(jnp.bfloat16)
    low = (rows - high.astype(jnp.float32)).astype(jnp.bfloat16)
    dot = functools.partial(jnp.dot, preferred_element_type=jnp.float32)
    return dot(high, high_ref[...]) + dot(low, high_ref[...]) + dot(high, low_ref[...])


def twiddles(shift_ref, middle_ref, twiddle_ref):
    shift = (shift_ref[0:1, :], shift_ref[1:2, :])
    twiddle_ref[0], twiddle_ref[1] = times((middle_ref[0], middle_ref[1]), shift)


def twiddle_row(twiddle_ref, index, sign):
    whole = (CHANS, LANES)
    real = jnp.broadcast_to(twiddle_ref[0, index : index + 1, :], whole)
    imag = jnp.broadcast_to(twiddle_ref[1, index : index + 1, :], whole)
    return (real, imag if sign > 0 else -imag)


def source(index):
    lanes = slice(index % TILES * LANES, (index % TILES + 1) * LANES)
    return index // TILES, lanes


def load(ref, index):
    return (ref[index, :, :LANES], ref[index, :, LANES:])


def store(ref, index, value):
    ref[index, :, :LANES], ref[index, :, LANES:] = value


def forward_kernel(
    mixed_ref, scalars_ref, shift_ref, middle_ref, high_ref, low_ref, spectrum_ref, work_ref, twiddle_ref
):
    twiddles(shift_ref, middle_ref, twiddle_ref)

    def scalar(index):
        return twiddle_row(scalars_ref, index, 1)

    for inner in range(8):
        values = []
        for outer in range(8):
            rank, lanes = source(8 * outer + inner)
            value = (mixed_ref[rank, 0, :, lanes], mixed_ref[rank, 1, :, lanes])
            values.append(times(value, scalar(outer)) if outer else value)
        values = dft8(values, -1)
        for a in range(8):
            store(work_ref, 8 * inner + a, times(values[a], scalar(8 + 8 * inner + a)) if inner else values[a])
    for a in range(8):
        values = dft8([load(work_ref, 8 * inner + a) for inner in range(8)], -1)
        for b in range(8):
            store(work_ref, 8 * b + a, times(values[b], twiddle_row(twiddle_ref, a + 8 * b, 1)))
    spectrum = product(work_ref[...].reshape(ROWS * CHANS, 2 * LANES), high_ref, low_ref)
    spectrum_ref[...] = spectrum.reshape(ROWS, CHANS, 2 * LANES)


def inverse_kernel(
    spectrum_ref, filter_ref, scalars_ref, shift_ref, middle_ref, high_ref, low_ref, out_ref, work_ref, twiddle_ref
):
    twiddles(shift_ref, middle_ref, twiddle_ref)

    def scalar(index):
        return twiddle_row(scalars_ref, index, -1)

    spectrum = spectrum_ref[...].reshape(ROWS * CHANS, 2 * LANES)
    filters = filter_ref[...].reshape(ROWS * CHANS, 2 * LANES)
    real, imag = times((spectrum[:, :LANES], spectrum[:, LANES:]), (filters[:, :LANES], -filters[:, LANES:]))
    back = product(jnp.concatenate([real, imag], axis=1), high_ref, low_ref)
    work_ref[...] = back.reshape(ROWS, CHANS, 2 * LANES)
    for a in range(8):
        values = []
        for b in range(8):
            values.append(times(load(work_ref, 8 * b + a), twiddle_row(twiddle_ref, a + 8 * b, -1)))
        values = dft8(values, 1)
        for inner in range(8):
            value = values[inner]
            store(work_ref, 8 * inner + a, times(value, scalar(8 + 8 * inner + a)) if inner else value)
    for inner in range(8):
        values = dft8([load(work_ref, 8 * inner + a) for a in range(8)], 1)
        for outer in range(8):
            real, imag = times(values[outer], scalar(outer)) if outer else values[outer]
            rank, lanes = source(8 * outer + inner)
            out_ref[rank, 0, :, lanes] = real
            out_ref[rank, 1, :, lanes] = imag


def term_kernel(rank_ref, spectrum_ref, saved_ref, keep_ref, send_ref):
    owners, rows = 2 * keep_ref.shape[0], keep_ref.shape[1] // 2
    rank = rank_ref[0]
    spectrum = spectrum_ref[...].reshape(ROWS * CHANS, 2 * LANES)
    saved = saved_ref[...].reshape(ROWS * CHANS, 2 * LANES)
    term = times((spectrum[:, :LANES], spectrum[:, LANES:]), (saved[:, :LANES], -saved[:, LANES:]))
    turned = [part.T for part in term]
    for pair in range(owners // 2):
        apart = rank >> 1 ^ pair
        slot = (apart >> 1 & 3) << 2 | apart >> 3 << 1 | apart & 1
        for part in range(2):
            place = slice(part * rows, (part + 1) * rows)
            even = turned[part][2 * pair * rows : (2 * pair + 1) * rows, :]
            odd = turned[part][(2 * pair + 1) * rows : (2 * pair + 2) * rows, :]
            keep_ref[slot, place, :] = jnp.where(rank & 1 == 0, even, odd)
            send_ref[slot, place, :] = jnp.where(rank & 1 == 0, odd, even)


def summed(total, sent):
    for array in sent:
        total = total + array
    return total


def sum_over_sequences(keep, send, owners):
    def swap(array, apart):
        return lax.ppermute(array, "dp", [(i, i ^ apart) for i in range(owners)])

    total = keep + swap(send, 1)
    total = total.reshape(4, 4, *keep.shape[1:])
    total = summed(total[0], [swap(total[k], (0, 4, 8, 12)[k]) for k in range(1, 4)])
    return summed(total[0], [swap(total[k], (0, 2, 16, 18)[k]) for k in range(1, 4)])


def call(kernel, outs, in_specs, scratch=()):
    specs = [pl.BlockSpec(memory_space=out.memory_space) for out in outs]
    return pl.pallas_call(
        kernel,
        out_shape=outs if len(outs) > 1 else outs[0],
        in_specs=in_specs,
        out_specs=specs if len(specs) > 1 else specs[0],
        scratch_shapes=list(scratch),
        interpret=INTERPRET,
    )


def leaving(shape, count):
    return [pltpu.VMEM(shape, jnp.float32), pltpu.SemaphoreType.DMA((count,))]


def on_chip(array):
    return array if INTERPRET else pltpu.with_memory_space_constraint(array, pltpu.VMEM)


def split_table(table):
    table = table.astype(np.float32)
    high = table.astype(jnp.bfloat16)
    low = (table - high.astype(np.float32)).astype(jnp.bfloat16)
    return high, low


def tables():
    lane = np.arange(LANES)
    angle = 2.0 * np.pi / LANES * (lane[:, None] * lane[None, :] % LANES)
    cosine, sine = np.cos(angle), np.sin(angle)
    there = np.block([[cosine, -sine], [sine, cosine]])
    back = np.block([[cosine, sine], [-sine, cosine]])
    middle_angle = -2.0 * np.pi / TOKENS * (np.arange(ROWS)[:, None] * lane[None, :])
    middle = np.stack([np.cos(middle_angle), np.sin(middle_angle)]).astype(np.float32)
    scalars = np.zeros((RANKS, 72, 2), np.float32)
    shift = np.zeros((RANKS, 2, LANES), np.float32)
    series = np.arange(8)
    for rank in range(RANKS):
        step = 4 * reversed_digits(rank) + 1
        outer = -2.0 * np.pi * step * 8 * series / 4096
        inner = -2.0 * np.pi * (step * series[:, None] / 4096 + series[:, None] * series[None, :] / 64)
        angles = np.concatenate([outer, inner.reshape(-1)])
        scalars[rank] = np.stack([np.cos(angles), np.sin(angles)], axis=1)
        lanes = -2.0 * np.pi * step * lane / (4 * LENGTH)
        shift[rank] = np.stack([np.cos(lanes), np.sin(lanes)])
    return split_table(there), split_table(back), middle, scalars, shift


def by_frequency(spectrum):
    parts = spectrum.reshape(CHANS, 2, LANES, ROWS)
    return jnp.transpose(parts, (3, 0, 1, 2)).reshape(ROWS, CHANS, 2 * LANES)


def per_device(output_gradient, input_spectrum, filter_spectrum):
    owners = lax.axis_size("dp")
    rank = lax.axis_index("ctx")
    there, back, middle, scalars, shift = tables()
    own = lambda table: lax.dynamic_index_in_dim(jnp.asarray(table), rank, 0, keepdims=False)
    exchange = lambda array, axis: lax.all_to_all(array, axis, split_axis=0, concat_axis=0, tiled=True)

    mixed_shape, block_shape = (RANKS, 2, CHANS, SLICE), (RANKS, CHANS, SLICE)
    slices = jnp.transpose(output_gradient.reshape(CHANS, RANKS, SLICE), (1, 0, 2))
    samples = exchange(slices, "ctx")
    filters = by_frequency(filter_spectrum)
    saved = by_frequency(input_spectrum[0])
    mixed = call(spread_kernel, [pltpu.HBM(mixed_shape, jnp.float32)], [VMEM], leaving(mixed_shape, TILES))(on_chip(samples))
    mixed = exchange(mixed, "ctx")
    work = (ROWS, CHANS, 2 * LANES)
    scratch = [pltpu.VMEM(work, jnp.float32), pltpu.VMEM((2, ROWS, LANES), jnp.float32)]
    scalars = on_chip(jnp.broadcast_to(own(scalars).T[:, :, None], (2, 72, LANES)))
    shift = on_chip(own(shift))
    middle = on_chip(jnp.asarray(middle))
    there, back = ([on_chip(jnp.asarray(table)) for table in pair] for pair in (there, back))
    spectrum = call(
        forward_kernel, [pltpu.VMEM(work, jnp.float32)], [VMEM] * 6, scratch
    )(on_chip(mixed), scalars, shift, middle, *there)
    half = pltpu.VMEM((owners // 2, 2 * LANES // owners, ROWS * CHANS), jnp.float32)
    keep, send = call(term_kernel, [half, half], [SMEM, VMEM, VMEM])(
        lax.axis_index("dp").reshape(1), on_chip(spectrum), on_chip(saved)
    )
    total = sum_over_sequences(keep, send, owners)
    parts = call(
        inverse_kernel,
        [pltpu.VMEM(mixed_shape, jnp.float32)],
        [VMEM] * 7,
        scratch,
    )(on_chip(spectrum), on_chip(filters), scalars, shift, middle, *back)
    parts = exchange(parts, "ctx")
    blocks = call(gather_kernel, [pltpu.HBM(block_shape, jnp.float32)], [VMEM], leaving(block_shape, TILES))(on_chip(parts))
    blocks = exchange(blocks, "ctx")
    blocks = blocks * (1.0 / LENGTH)
    input_gradient = jnp.transpose(blocks, (1, 0, 2)).reshape(1, CHANS, TOKENS)
    total = total.reshape(2, LANES // owners, ROWS, CHANS)
    filter_gradient = jnp.transpose(total, (3, 0, 1, 2)).reshape(CHANS, 2, TOKENS // owners)
    return (input_gradient, filter_gradient)


def solution(mesh):
    in_specs = (P("dp", None, "ctx"), P("dp", None, None, "ctx"), P(None, None, "ctx"))
    out_specs = (P("dp", None, "ctx"), P(None, None, ("ctx", "dp")))
    return jax.shard_map(
        per_device, mesh=mesh, in_specs=in_specs, out_specs=out_specs, check_vma=False
    )
```

```python
import functools
import math

import jax
import jax.numpy as jnp
import numpy as np
from jax import lax
from jax.experimental import pallas as pl
from jax.experimental.pallas import tpu as pltpu
from jax.sharding import PartitionSpec as P

INTERPRET = False
RANKS = 16
CHANS = 8
LANES = 128
ROWS = 64
TOKENS = ROWS * LANES
LENGTH = RANKS * TOKENS
SLICE = TOKENS // RANKS
TILES = SLICE // LANES

VMEM = pl.BlockSpec(memory_space=pltpu.VMEM)
SMEM = pl.BlockSpec(memory_space=pltpu.SMEM)


def reversed_digits(index, sections=4):
    return sum((index >> level & 1) << sections - 1 - level for level in range(sections))


def rotor(angle_over_circle):
    angle = 2.0 * math.pi * angle_over_circle
    return (math.cos(angle), math.sin(angle))


def times(value, factor):
    real, imag = value
    cosine, sine = factor
    return (real * cosine - imag * sine, real * sine + imag * cosine)


def plus(left, right):
    return (left[0] + right[0], left[1] + right[1])


def minus(left, right):
    return (left[0] - right[0], left[1] - right[1])


def quarter(value, sign):
    real, imag = value
    return (-imag, real) if sign > 0 else (imag, -real)


def dft4(values, sign):
    even_sum, even_diff = plus(values[0], values[2]), minus(values[0], values[2])
    odd_sum, odd_diff = plus(values[1], values[3]), minus(values[1], values[3])
    turned = quarter(odd_diff, sign)
    return [plus(even_sum, odd_sum), plus(even_diff, turned), minus(even_sum, odd_sum), minus(even_diff, turned)]


def dft8(values, sign):
    even = dft4(values[0::2], sign)
    odd = dft4(values[1::2], sign)
    half = math.sqrt(0.5)
    real, imag = odd[1]
    one = ((real - imag) * half, (real + imag) * half) if sign > 0 else ((real + imag) * half, (imag - real) * half)
    real, imag = odd[3]
    three = ((-real - imag) * half, (real - imag) * half) if sign > 0 else ((imag - real) * half, (-real - imag) * half)
    odd = [odd[0], one, quarter(odd[2], sign), three]
    return [plus(even[k], odd[k]) for k in range(4)] + [minus(even[k], odd[k]) for k in range(4)]


def spread_kernel(samples_ref, sent_ref, out_ref, semaphores):
    copies = []
    for tile in range(TILES):
        lanes = slice(tile * LANES, (tile + 1) * LANES)
        first = []
        for low in range(4):
            turned = []
            for high in range(4):
                sample = samples_ref[4 * high + low, :, lanes]
                cosine, sine = rotor(-high / 16)
                turned.append((sample * cosine, sample * sine))
            turned[0] = (samples_ref[low, :, lanes], jnp.zeros((CHANS, LANES), jnp.float32))
            first.append(dft4(turned, -1))
        for residue in range(4):
            last = [first[0][residue]] + [
                times(first[low][residue], rotor(-(4 * residue + 1) * low / 64)) for low in range(1, 4)
            ]
            for high, (real, imag) in enumerate(dft4(last, -1)):
                owner = reversed_digits(4 * high + residue)
                out_ref[owner, 0, :, lanes] = real
                out_ref[owner, 1, :, lanes] = imag
        where = (slice(None), slice(None), slice(None), lanes)
        copies.append(pltpu.make_async_copy(out_ref.at[where], sent_ref.at[where], semaphores.at[tile]))
        copies[-1].start()
    for copy in copies:
        copy.wait()


def gather_kernel(parts_ref, sent_ref, out_ref, semaphores):
    copies = []
    for tile in range(TILES):
        lanes = slice(tile * LANES, (tile + 1) * LANES)
        first = []
        for residue in range(4):
            owners = [reversed_digits(4 * high + residue) for high in range(4)]
            values = dft4([(parts_ref[o, 0, :, lanes], parts_ref[o, 1, :, lanes]) for o in owners], 1)
            first.append(
                [values[0]] + [times(values[low], rotor((4 * residue + 1) * low / 64)) for low in range(1, 4)]
            )
        for low in range(4):
            values = dft4([first[residue][low] for residue in range(4)], 1)
            for high in range(4):
                cosine, sine = rotor(high / 16)
                real, imag = values[high]
                out_ref[4 * high + low, :, lanes] = real if high == 0 else real * cosine - imag * sine
        where = (slice(None), slice(None), lanes)
        copies.append(pltpu.make_async_copy(out_ref.at[where], sent_ref.at[where], semaphores.at[tile]))
        copies[-1].start()
    for copy in copies:
        copy.wait()


def product(rows, high_ref, low_ref):
    high = rows.astype(jnp.bfloat16)
    low = (rows - high.astype(jnp.float32)).astype(jnp.bfloat16)
    dot = functools.partial(jnp.dot, preferred_element_type=jnp.float32)
    return dot(high, high_ref[...]) + dot(low, high_ref[...]) + dot(high, low_ref[...])


def twiddles(shift_ref, middle_ref, twiddle_ref):
    shift = (shift_ref[0:1, :], shift_ref[1:2, :])
    twiddle_ref[0], twiddle_ref[1] = times((middle_ref[0], middle_ref[1]), shift)


def twiddle_row(twiddle_ref, index, sign):
    whole = (CHANS, LANES)
    real = jnp.broadcast_to(twiddle_ref[0, index : index + 1, :], whole)
    imag = jnp.broadcast_to(twiddle_ref[1, index : index + 1, :], whole)
    return (real, imag if sign > 0 else -imag)


def source(index):
    lanes = slice(index % TILES * LANES, (index % TILES + 1) * LANES)
    return index // TILES, lanes


def load(ref, index):
    return (ref[index, :, :LANES], ref[index, :, LANES:])


def store(ref, index, value):
    ref[index, :, :LANES], ref[index, :, LANES:] = value


def forward_kernel(
    mixed_ref, scalars_ref, shift_ref, middle_ref, high_ref, low_ref, spectrum_ref, work_ref, twiddle_ref
):
    twiddles(shift_ref, middle_ref, twiddle_ref)

    def scalar(index):
        return twiddle_row(scalars_ref, index, 1)

    for inner in range(8):
        values = []
        for outer in range(8):
            rank, lanes = source(8 * outer + inner)
            value = (mixed_ref[rank, 0, :, lanes], mixed_ref[rank, 1, :, lanes])
            values.append(times(value, scalar(outer)) if outer else value)
        values = dft8(values, -1)
        for a in range(8):
            store(work_ref, 8 * inner + a, times(values[a], scalar(8 + 8 * inner + a)) if inner else values[a])
    for a in range(8):
        values = dft8([load(work_ref, 8 * inner + a) for inner in range(8)], -1)
        for b in range(8):
            store(work_ref, 8 * b + a, times(values[b], twiddle_row(twiddle_ref, a + 8 * b, 1)))
    spectrum = product(work_ref[...].reshape(ROWS * CHANS, 2 * LANES), high_ref, low_ref)
    spectrum_ref[...] = spectrum.reshape(ROWS, CHANS, 2 * LANES)


def inverse_kernel(
    spectrum_ref, filter_ref, scalars_ref, shift_ref, middle_ref, high_ref, low_ref, sent_ref, work_ref, twiddle_ref,
    out_ref, semaphores,
):
    twiddles(shift_ref, middle_ref, twiddle_ref)

    def scalar(index):
        return twiddle_row(scalars_ref, index, -1)

    spectrum = spectrum_ref[...].reshape(ROWS * CHANS, 2 * LANES)
    filters = filter_ref[...].reshape(ROWS * CHANS, 2 * LANES)
    real, imag = times((spectrum[:, :LANES], spectrum[:, LANES:]), (filters[:, :LANES], -filters[:, LANES:]))
    back = product(jnp.concatenate([real, imag], axis=1), high_ref, low_ref)
    work_ref[...] = back.reshape(ROWS, CHANS, 2 * LANES)
    for a in range(8):
        values = []
        for b in range(8):
            values.append(times(load(work_ref, 8 * b + a), twiddle_row(twiddle_ref, a + 8 * b, -1)))
        values = dft8(values, 1)
        for inner in range(8):
            value = values[inner]
            store(work_ref, 8 * inner + a, times(value, scalar(8 + 8 * inner + a)) if inner else value)
    copies = []
    for inner in range(8):
        values = dft8([load(work_ref, 8 * inner + a) for a in range(8)], 1)
        for outer in range(8):
            real, imag = times(values[outer], scalar(outer)) if outer else values[outer]
            lanes = slice(inner % TILES * LANES, (inner % TILES + 1) * LANES)
            out_ref[outer, inner // TILES, 0, :, lanes] = real
            out_ref[outer, inner // TILES, 1, :, lanes] = imag
        if inner % TILES == TILES - 1:
            half = inner // TILES
            copies.append(pltpu.make_async_copy(out_ref.at[:, half], sent_ref.at[:, half], semaphores.at[half]))
            copies[-1].start()
    for copy in copies:
        copy.wait()


def term_kernel(rank_ref, spectrum_ref, saved_ref, keep_ref, send_ref):
    owners, rows = 2 * keep_ref.shape[0], keep_ref.shape[1] // 2
    rank = rank_ref[0]
    spectrum = spectrum_ref[...].reshape(ROWS * CHANS, 2 * LANES)
    saved = saved_ref[...].reshape(ROWS * CHANS, 2 * LANES)
    term = times((spectrum[:, :LANES], spectrum[:, LANES:]), (saved[:, :LANES], -saved[:, LANES:]))
    turned = [part.T for part in term]
    side = rank >> 1 & 1
    for pair in range(owners // 2):
        first = pair >> 1 << 2 | pair & 1
        apart = (rank ^ first) & ~2
        slot = (apart >> 2 & 3) << 2 | apart >> 4 << 1 | apart & 1
        for part in range(2):
            place = slice(part * rows, (part + 1) * rows)
            even = turned[part][first * rows : (first + 1) * rows, :]
            odd = turned[part][(first + 2) * rows : (first + 3) * rows, :]
            keep_ref[slot, place, :] = jnp.where(side == 0, even, odd)
            send_ref[slot, place, :] = jnp.where(side == 0, odd, even)


def summed(total, sent):
    for array in sent:
        total = total + array
    return total


def sum_over_sequences(keep, send, owners):
    def swap(array, apart):
        return lax.ppermute(array, "dp", [(i, i ^ apart) for i in range(owners)])

    total = keep + swap(send, 2)
    total = total.reshape(4, 4, *keep.shape[1:])
    total = summed(total[0], [swap(total[k], (0, 4, 8, 12)[k]) for k in range(1, 4)])
    return summed(total[0], [swap(total[k], (0, 1, 16, 17)[k]) for k in range(1, 4)])


def call(kernel, outs, in_specs, scratch=()):
    specs = [pl.BlockSpec(memory_space=out.memory_space) for out in outs]
    return pl.pallas_call(
        kernel,
        out_shape=outs if len(outs) > 1 else outs[0],
        in_specs=in_specs,
        out_specs=specs if len(specs) > 1 else specs[0],
        scratch_shapes=list(scratch),
        interpret=INTERPRET,
    )


def leaving(shape, count):
    return [pltpu.VMEM(shape, jnp.float32), pltpu.SemaphoreType.DMA((count,))]


def on_chip(array):
    return array if INTERPRET else pltpu.with_memory_space_constraint(array, pltpu.VMEM)


def split_table(table):
    table = table.astype(np.float32)
    high = table.astype(jnp.bfloat16)
    low = (table - high.astype(np.float32)).astype(jnp.bfloat16)
    return high, low


def tables():
    lane = np.arange(LANES)
    angle = 2.0 * np.pi / LANES * (lane[:, None] * lane[None, :] % LANES)
    cosine, sine = np.cos(angle), np.sin(angle)
    there = np.block([[cosine, -sine], [sine, cosine]])
    back = np.block([[cosine, sine], [-sine, cosine]])
    middle_angle = -2.0 * np.pi / TOKENS * (np.arange(ROWS)[:, None] * lane[None, :])
    middle = np.stack([np.cos(middle_angle), np.sin(middle_angle)]).astype(np.float32)
    scalars = np.zeros((RANKS, 72, 2), np.float32)
    shift = np.zeros((RANKS, 2, LANES), np.float32)
    series = np.arange(8)
    for rank in range(RANKS):
        step = 4 * reversed_digits(rank) + 1
        outer = -2.0 * np.pi * step * 8 * series / 4096
        inner = -2.0 * np.pi * (step * series[:, None] / 4096 + series[:, None] * series[None, :] / 64)
        angles = np.concatenate([outer, inner.reshape(-1)])
        scalars[rank] = np.stack([np.cos(angles), np.sin(angles)], axis=1)
        lanes = -2.0 * np.pi * step * lane / (4 * LENGTH)
        shift[rank] = np.stack([np.cos(lanes), np.sin(lanes)])
    return split_table(there), split_table(back), middle, scalars, shift


def by_frequency(spectrum):
    parts = spectrum.reshape(CHANS, 2, LANES, ROWS)
    return jnp.transpose(parts, (3, 0, 1, 2)).reshape(ROWS, CHANS, 2 * LANES)


def per_device(output_gradient, input_spectrum, filter_spectrum):
    owners = lax.axis_size("dp")
    rank = lax.axis_index("ctx")
    there, back, middle, scalars, shift = tables()
    own = lambda table: lax.dynamic_index_in_dim(jnp.asarray(table), rank, 0, keepdims=False)
    exchange = lambda array, axis: lax.all_to_all(array, axis, split_axis=0, concat_axis=0, tiled=True)

    half_shape = (RANKS // 2, 2, 2, CHANS, SLICE)
    mixed_shape, block_shape = (RANKS, 2, CHANS, SLICE), (RANKS, CHANS, SLICE)
    slices = jnp.transpose(output_gradient.reshape(CHANS, RANKS, SLICE), (1, 0, 2))
    samples = exchange(slices, "ctx")
    filters = by_frequency(filter_spectrum)
    saved = by_frequency(input_spectrum[0])
    mixed = call(spread_kernel, [pltpu.HBM(mixed_shape, jnp.float32)], [VMEM], leaving(mixed_shape, TILES))(on_chip(samples))
    mixed = exchange(mixed, "ctx")
    work = (ROWS, CHANS, 2 * LANES)
    scratch = [pltpu.VMEM(work, jnp.float32), pltpu.VMEM((2, ROWS, LANES), jnp.float32)]
    scalars = on_chip(jnp.broadcast_to(own(scalars).T[:, :, None], (2, 72, LANES)))
    shift = on_chip(own(shift))
    middle = on_chip(jnp.asarray(middle))
    there, back = ([on_chip(jnp.asarray(table)) for table in pair] for pair in (there, back))
    spectrum = call(
        forward_kernel, [pltpu.VMEM(work, jnp.float32)], [VMEM] * 6, scratch
    )(on_chip(mixed), scalars, shift, middle, *there)
    half = pltpu.VMEM((owners // 2, 2 * LANES // owners, ROWS * CHANS), jnp.float32)
    keep, send = call(term_kernel, [half, half], [SMEM, VMEM, VMEM])(
        lax.axis_index("dp").reshape(1), on_chip(spectrum), on_chip(saved)
    )
    total = sum_over_sequences(keep, send, owners)
    parts = call(
        inverse_kernel,
        [pltpu.HBM(half_shape, jnp.float32)],
        [VMEM] * 7,
        scratch + leaving(half_shape, 2),
    )(on_chip(spectrum), on_chip(filters), scalars, shift, middle, *back).reshape(mixed_shape)
    parts = exchange(parts, "ctx")
    blocks = call(gather_kernel, [pltpu.HBM(block_shape, jnp.float32)], [VMEM], leaving(block_shape, TILES))(on_chip(parts))
    blocks = exchange(blocks, "ctx")
    blocks = blocks * (1.0 / LENGTH)
    input_gradient = jnp.transpose(blocks, (1, 0, 2)).reshape(1, CHANS, TOKENS)
    total = total.reshape(2, LANES // owners, ROWS, CHANS)
    filter_gradient = jnp.transpose(total, (3, 0, 1, 2)).reshape(CHANS, 2, TOKENS // owners)
    return (input_gradient, filter_gradient)


def solution(mesh):
    in_specs = (P("dp", None, "ctx"), P("dp", None, None, "ctx"), P(None, None, "ctx"))
    out_specs = (P("dp", None, "ctx"), P(None, None, ("ctx", "dp")))
    return jax.shard_map(
        per_device, mesh=mesh, in_specs=in_specs, out_specs=out_specs, check_vma=False
    )
```
